512 devices in a mesh: dp: 16 (over y_hi, z), blk: 32 (over x, y_lo, core).
Axes of the slice: x: 4, y: 8 (y_hi: 2, y_lo: 4; y = y_hi * 4 + y_lo), z: 8, core: 2. Of those that a mesh axis runs over, the one named last changes fastest.
Arguments:
- queries: bfloat16 [65536, 2048], P(('dp', 'blk')), may hold values from -54 to 54
- keys: bfloat16 [4096, 2048], P(('dp', 'blk')), may hold values from -7 to 7
- memory_values: bfloat16 [4096, 2048], P(('dp', 'blk')), may hold values from -6 to 6
- block_mask: int32 [1024, 32], P(('dp', 'blk')), may hold values from 0 to 1, as said below
- head_gate: float32 [16], replicated, may hold values from 0.5 to 2
- out_grad: bfloat16 [65536, 2048], P(('dp', 'blk')), may hold values from -6 to 6
Outputs:
- attended: bfloat16 [65536, 2048], P(('dp', 'blk'))
- query_gradient: bfloat16 [65536, 2048], P(('dp', 'blk'))
- key_gradient: float32 [4096, 2048], P(('dp', 'blk'))
- value_gradient: float32 [4096, 2048], P(('dp', 'blk'))
- gate_grad: float32 [16], replicated
The draws below stay inside these ranges and needn't reach their ends.
Inputs may be any that keep to these rules, and one draw needn't show every extreme that they name: `block_mask`: every row has at least one 1. Column b stands for the memory rows of block b of the row's batch.
All inputs are finite; a program needn't handle non-finite values.
Results may differ from the reference program's by a relative error of at most 0.02.
Values may be sent and summed in bfloat16 or wider, within the bound.
A program may use at most 64 MiB of HBM per device.

```python
import functools
import math
import jax
import jax.numpy as jnp
from jax import lax

HEADS = 16
HEAD_DIM = 128
QBLK = 64
TQ = 128
TM = 8
HEAD_FEATURES = 2048
TOKENS = 65536
MEMORY = 4096
N_DP = 16
N_BLK = 32


def mask_parts(key):
    block_count = TOKENS // QBLK
    per_device = TQ // QBLK
    levels = jax.random.randint(jax.random.fold_in(key, 101), (N_DP * N_BLK,), 1, 9)
    row_levels = jnp.repeat(levels, per_device)
    random_bits = jax.random.randint(jax.random.fold_in(key, 102), (block_count, N_BLK), 0, 8)
    home_block = jax.random.randint(jax.random.fold_in(key, 103), (block_count,), 0, N_BLK)
    column_ids = jnp.arange(N_BLK)[None, :]
    allowed = (random_bits < row_levels[:, None]) | (column_ids == home_block[:, None])
    return allowed.astype(jnp.int32)


def key_parts(key):
    drawn = jax.random.truncated_normal(jax.random.fold_in(key, 111), -6.0, 6.0, (MEMORY, HEAD_FEATURES), jnp.float32)
    return drawn


def draw_keys(key, part):
    return key_parts(key).astype(jnp.bfloat16)


def draw_queries(key, part):
    drawn = jax.random.truncated_normal(jax.random.fold_in(key, 121), -6.0, 6.0, (TOKENS, HEAD_FEATURES), jnp.float32)
    return drawn.astype(jnp.bfloat16)


def draw_block_mask(key, part):
    return mask_parts(key)


def block_scale(stream_key, extent, cuts, smallest, high):
    level = 1.0
    for axis_at, blocks in cuts:
        draws = jax.random.uniform(jax.random.fold_in(jax.random.fold_in(stream_key, 6), axis_at), (blocks,), jnp.float32, smallest / len(cuts), high / len(cuts))
        level = level * jnp.repeat(jnp.exp(draws), extent[axis_at] // blocks).reshape((-1,) + (1,) * (len(extent) - 1 - axis_at))
    return level


def centred(own_key, shape, scale, limit, pieces=(), kind=jnp.bfloat16):
    factor_of = block_scale(own_key, shape, pieces, -0.22, 0.18) if pieces else 1.0
    array = jax.random.normal(own_key, shape, jnp.float32) * scale * factor_of
    return jnp.minimum(jnp.maximum(array, -limit), limit).astype(kind)


def setup_inputs(seed: int = 0) -> dict:
    key_of = jax.random.split(jax.random.key(seed), 7)
    return {
        "queries": draw_queries(jax.random.fold_in(key_of[6], 71), 0),
        "keys": draw_keys(jax.random.fold_in(key_of[6], 71), 0),
        "memory_values": centred(key_of[2], (MEMORY, HEAD_FEATURES), 1.0, 6.0, ((0, 512),)),
        "block_mask": draw_block_mask(jax.random.fold_in(key_of[6], 71), 0),
        "head_gate": jnp.clip(jax.random.uniform(key_of[4], (HEADS,), jnp.float32, 0.5, 2.0), 0.5, 2.0),
        "out_grad": centred(key_of[5], (TOKENS, HEAD_FEATURES), 1.0, 6.0, ((0, 512),)),
    }


def group_pass(head_gate, packed):
    query_rows, key_rows, value_rows, block_rows, grad_rows = packed
    score_scale = 1.0 / math.sqrt(HEAD_DIM)
    split_query_heads = query_rows.astype(jnp.float32).reshape(-1, HEADS, HEAD_DIM)
    split_key_heads = key_rows.astype(jnp.float32).reshape(-1, HEADS, HEAD_DIM)
    split_value_heads = value_rows.astype(jnp.float32).reshape(-1, HEADS, HEAD_DIM)
    allowed = jnp.repeat(jnp.repeat(block_rows, QBLK, axis=0), TM, axis=1) > 0
    logit_scores = jnp.einsum('bes,fes->ebf', split_query_heads, split_key_heads) * score_scale
    logit_scores = jnp.where(allowed[None], logit_scores, jnp.float32(-1e+30))
    largest = lax.optimization_barrier(jnp.max(logit_scores, axis=2, keepdims=True))
    raised = jnp.exp(logit_scores - largest)
    totals = lax.optimization_barrier(jnp.sum(raised, axis=2, keepdims=True))
    probs = raised / totals
    narrow_probabilities = lax.optimization_barrier(probs.astype(jnp.bfloat16))
    output_heads = jnp.einsum('bzf,fbs->zbs', narrow_probabilities.astype(jnp.float32), split_value_heads)
    attended = (head_gate[None, :, None] * output_heads).astype(jnp.bfloat16).reshape(-1, HEAD_FEATURES)
    grad_heads = grad_rows.astype(jnp.float32).reshape(-1, HEADS, HEAD_DIM)
    gate_part = lax.optimization_barrier(jnp.sum(grad_heads * output_heads, axis=(0, 2)))
    scaled_grad = head_gate[None, :, None] * grad_heads
    narrow_scaled_scores = lax.optimization_barrier(scaled_grad.astype(jnp.bfloat16))
    deltas = lax.optimization_barrier(jnp.sum(scaled_grad * output_heads, axis=2))
    probability_gradient = jnp.einsum('bes,fes->ebf', narrow_scaled_scores.astype(jnp.float32), split_value_heads)
    score_grads = probs * (probability_gradient - jnp.transpose(deltas)[:, :, None]) * score_scale
    narrow_scores = lax.optimization_barrier(score_grads.astype(jnp.bfloat16)).astype(jnp.float32)
    query_gradient = jnp.einsum('bzf,fbs->zbs', narrow_scores, split_key_heads).astype(jnp.bfloat16).reshape(-1, HEAD_FEATURES)
    key_gradient = jnp.einsum('yor,oyt->ryt', narrow_scores, split_query_heads).reshape(-1, HEAD_FEATURES)
    value_gradient = jnp.einsum('yor,oyt->ryt', narrow_probabilities.astype(jnp.float32), narrow_scaled_scores.astype(jnp.float32)).reshape(-1, HEAD_FEATURES)
    return (attended, query_gradient, key_gradient, value_gradient, gate_part)

def reference(queries, keys, memory_values, block_mask, head_gate, out_grad):
    group_queries = TQ * N_BLK
    group_memory = TM * N_BLK
    packed = (queries.reshape(N_DP, group_queries, HEAD_FEATURES), keys.reshape(N_DP, group_memory, HEAD_FEATURES), memory_values.reshape(N_DP, group_memory, HEAD_FEATURES), block_mask.reshape(N_DP, group_queries // QBLK, N_BLK), out_grad.reshape(N_DP, group_queries, HEAD_FEATURES))
    attended, query_gradient, key_gradient, value_gradient, gate_parts = lax.map(functools.partial(group_pass, head_gate), packed)
    gate_grad = lax.optimization_barrier(jnp.sum(gate_parts, axis=0)) / math.sqrt(TOKENS * HEAD_DIM)
    return (attended.reshape(TOKENS, HEAD_FEATURES), query_gradient.reshape(TOKENS, HEAD_FEATURES), key_gradient.reshape(MEMORY, HEAD_FEATURES), value_gradient.reshape(MEMORY, HEAD_FEATURES), gate_grad)
```

```python
import math

import jax
import jax.numpy as jnp
from jax import lax
from jax.experimental import pallas as pl
from jax.experimental.pallas import tpu as pltpu
from jax.sharding import PartitionSpec as P

MESH = pl.DeviceIdType.MESH
HEADS, HEAD_DIM, QBLK = 16, 128, 64
TQ, TM, FEAT = 128, 8, 2048
NX, NY, NZ, NYL = 4, 8, 8, 4
HALF = FEAT // 2
CHUNKS = 2
CH_HEADS = HEADS // 2 // CHUNKS
CW = CH_HEADS * HEAD_DIM
CHIPS = NX * NYL
ROWS = 2 * TM
MEM = CHIPS * ROWS
NQ = 2 * TQ
SEMS = 80
BF, F32 = jnp.bfloat16, jnp.float32


def nt(a, b):
    return lax.dot_general(a, b, (((1,), (1,)), ((), ())), preferred_element_type=F32)


def tn(a, b):
    return lax.dot_general(a, b, (((0,), (0,)), ((), ())), preferred_element_type=F32)


def nn(a, b):
    return lax.dot_general(a, b, (((1,), (0,)), ((), ())), preferred_element_type=F32)


def kernel(
    q_ref, k_ref, v_ref, mask_ref, gate_ref, og_ref,
    att_out, qg_out, kg_out, vg_out, gg_out,
    kx, vx, qa, oa, mb, bias, gath, att, qg, term, rxa, rxn, ysum, yrx, fin, gsl, send, recv, local,
):
    dp, blk = lax.axis_index("dp"), lax.axis_index("blk")
    y_hi, z = dp // NZ, dp % NZ
    x, y_lo, c = blk // (2 * NYL), (blk // 2) % NYL, blk % 2
    y = y_hi * NYL + y_lo
    me = x * NYL + y_lo

    def device(x=x, y=y, z=z, c=c):
        return (y // NYL * NZ + z, x * (2 * NYL) + (y % NYL) * 2 + c)

    partner = device(c=1 - c)
    right, left = device(x=(x + 1) % NX), device(x=(x + NX - 1) % NX)
    y_near = [device(y=y_hi * NYL + (y_lo + d) % NYL) for d in range(1, NYL)]
    gate_peers = [
        [device(x=(x + d) % NX) for d in range(1, NX)],
        [device(y=(y + d) % NY) for d in range(1, NY)],
        [device(z=(z + d) % NZ) for d in range(1, NZ)],
        [partner],
    ]

    count = [0, 0]
    sent, stayed = [], []

    def remote(src, dst, to):
        i = count[0]
        count[0] += 1
        copy = pltpu.make_async_remote_copy(
            src_ref=src, dst_ref=dst, send_sem=send.at[i], recv_sem=recv.at[i],
            device_id=to, device_id_type=MESH,
        )
        copy.start()
        sent.append(copy)
        return copy

    def stay(src, dst):
        i = count[1]
        count[1] += 1
        copy = pltpu.make_async_copy(src, dst, local.at[i])
        copy.start()
        return copy

    mine = pl.ds(pl.multiple_of(c * HALF, HALF), HALF)
    other = pl.ds(pl.multiple_of((1 - c) * HALF, HALF), HALF)

    own_kv = [stay(k_ref.at[:, mine], kx.at[c]), stay(v_ref.at[:, mine], vx.at[c])]
    own_q = [stay(q_ref.at[:, mine], qa.at[0]), stay(og_ref.at[:, mine], oa.at[0])]
    mb[0] = jnp.zeros((8, 128), F32)
    mb[0, 0:2, 0 : 2 * CHIPS] = mask_ref[...].astype(F32)

    barrier = pltpu.get_barrier_semaphore()
    peers = [to for stage in gate_peers for to in stage]
    for to in peers:
        pl.semaphore_signal(barrier, inc=1, device_id=to, device_id_type=MESH)
    pl.semaphore_wait(barrier, len(peers))

    kv_in = [
        remote(k_ref.at[:, other], kx.at[c], partner),
        remote(v_ref.at[:, other], vx.at[c], partner),
    ]
    mask_in = remote(mb.at[0], mb.at[1], partner)
    q_in = [
        remote(q_ref.at[:, other], qa.at[1], partner),
        remote(og_ref.at[:, other], oa.at[1], partner),
    ]

    for copy in own_kv:
        copy.wait()
    for copy in kv_in:
        copy.wait_recv()
    k_rows = kx[...].astype(F32).reshape(ROWS, HALF).astype(BF)
    v_rows = vx[...].astype(F32).reshape(ROWS, HALF).astype(BF)
    for j in range(CHUNKS):
        gath[j, me, :, 0:CW] = k_rows[:, j * CW : (j + 1) * CW]
        gath[j, me, :, CW : 2 * CW] = v_rows[:, j * CW : (j + 1) * CW]

    y_in = [
        [remote(gath.at[j, me], gath.at[j, me], to) for to in y_near] for j in range(CHUNKS)
    ]

    mask_in.wait_recv()
    rows = lax.broadcasted_iota(jnp.int32, (MEM, 128), 0) // TM
    lanes = lax.broadcasted_iota(jnp.int32, (MEM, 128), 1)
    pick = jnp.where(rows == lanes, 1.0, 0.0).astype(F32)
    spread = jnp.concatenate(
        [jnp.broadcast_to(mb[s, b : b + 1, :], (QBLK, 128)) for s in range(2) for b in range(2)],
        axis=0,
    )
    bias[...] = (nt(pick.astype(BF), spread.astype(BF)) - 1.0) * 1e30

    x_of = lambda d: (x + d) % NX
    x_in = []
    for j in range(CHUNKS):
        for copy in y_in[j]:
            copy.wait_recv()
        block = gath.at[j, pl.ds(x * NYL, NYL)]
        x_in.append([remote(block, block, right), remote(block, block, left)])
    far_in = []
    for j in range(CHUNKS):
        x_in[j][0].wait_recv()
        part = gath.at[j, pl.ds(x_of(3) * NYL, 2)]
        first = remote(part, part, right)
        x_in[j][1].wait_recv()
        part = gath.at[j, pl.ds(x_of(1) * NYL + 2, 2)]
        far_in.append([first, remote(part, part, left)])

    for copy in own_q:
        copy.wait()
    for copy in q_in:
        copy.wait_recv()

    scale = 1.0 / math.sqrt(HEAD_DIM)
    lane = lax.broadcasted_iota(jnp.int32, (8, 128), 1)
    gate_row = jnp.zeros((8, 128), F32)
    rx1 = []
    for j in range(CHUNKS):
        for copy in far_in[j]:
            copy.wait_recv()
        for h in range(CH_HEADS):
            head = j * CH_HEADS + h
            cols = slice(head * HEAD_DIM, (head + 1) * HEAD_DIM)
            kc = slice(h * HEAD_DIM, (h + 1) * HEAD_DIM)
            vc = slice(CW + h * HEAD_DIM, CW + (h + 1) * HEAD_DIM)
            g = gate_ref[c * (HEADS // 2) + head]
            qh = qa[:, :, cols].reshape(NQ, HEAD_DIM)
            oh = oa[:, :, cols].reshape(NQ, HEAD_DIM)
            kh = gath[j, :, :, kc].reshape(MEM, HEAD_DIM)
            vh = gath[j, :, :, vc].reshape(MEM, HEAD_DIM)
            s = nt(kh, qh) * (scale * math.log2(math.e)) + bias[...]
            e = jnp.exp2(s - jnp.max(s, axis=0, keepdims=True))
            p = e * (1.0 / jnp.sum(e, axis=0, keepdims=True))
            low = p.astype(BF)
            dp_ = nt(vh, oh)
            delta = jnp.sum(low.astype(F32) * dp_, axis=0, keepdims=True)
            ds = (p * (dp_ - delta) * (g * scale)).astype(BF)
            term[j, :, :, kc] = nn(ds, qh).astype(BF).reshape(CHIPS, ROWS, HEAD_DIM)
            term[j, :, :, vc] = (nn(low, oh) * g).astype(BF).reshape(CHIPS, ROWS, HEAD_DIM)
            att[:, :, cols] = (tn(low, vh) * g).astype(BF).reshape(2, TQ, HEAD_DIM)
            qg[:, :, cols] = tn(ds, kh).astype(BF).reshape(2, TQ, HEAD_DIM)
            total = jnp.sum(delta, axis=1, keepdims=True)
            gate_row = gate_row + jnp.where(lane == c * (HEADS // 2) + head, total, 0.0)
        rx1.append([
            remote(term.at[j, pl.ds(x_of(2) * NYL, 2)], rxa.at[j, 0], right),
            remote(term.at[j, pl.ds(x_of(2) * NYL + 2, 2)], rxa.at[j, 1], left),
        ])

    rx2 = []

    def reduce_x(j):
        rx1[j][0].wait_recv()
        to = pl.ds(x_of(1) * NYL, 2)
        term[j, to] = (term[j, to].astype(F32) + rxa[j, 0].astype(F32)).astype(BF)
        first = remote(term.at[j, pl.ds(x_of(1) * NYL, NYL)], rxn.at[j, 0], right)
        rx1[j][1].wait_recv()
        to = pl.ds(x_of(3) * NYL + 2, 2)
        term[j, to] = (term[j, to].astype(F32) + rxa[j, 1].astype(F32)).astype(BF)
        rx2.append([first, remote(term.at[j, pl.ds(x_of(3) * NYL, NYL)], rxn.at[j, 1], left)])

    gate_slots = [(0, NX, x), (NX, NY, y), (NX + NY, NZ, z), (NX + NY + NZ, 2, c)]
    gate_in = []

    def gate_send(stage, row):
        base, _, at = gate_slots[stage]
        gsl[base + at] = row
        for to in gate_peers[stage]:
            gate_in.append(remote(gsl.at[base + at], gsl.at[base + at], to))

    def gate_take(stage):
        base, size, _ = gate_slots[stage]
        for copy in gate_in:
            copy.wait_recv()
        gate_in.clear()
        row = gsl[base]
        for i in range(1, size):
            row = row + gsl[base + i]
        return row

    gate_send(0, gate_row)
    reduce_x(0)
    ends = []

    def put(src, out, j):
        lo = pl.ds(pl.multiple_of(c * HALF + j * CW, CW), CW)
        part = slice(j * CW, (j + 1) * CW)
        ends.append(remote(src.at[1, :, part], out.at[:, lo], partner))
        stayed.append(stay(src.at[0, :, part], out.at[:, lo]))

    reduce_x(1)
    for j in range(CHUNKS):
        put(att, att_out, j)
        put(qg, qg_out, j)
    gate_send(1, gate_take(0))

    ry = []
    for j in range(CHUNKS):
        for copy in rx2[j]:
            copy.wait_recv()
        own = term[j, pl.ds(x * NYL, NYL)].astype(F32)
        ysum[j] = (own + rxn[j, 0].astype(F32) + rxn[j, 1].astype(F32)).astype(BF)
        ry.append([
            remote(ysum.at[j, (y_lo + d) % NYL], yrx.at[j, d - 1], y_near[d - 1])
            for d in range(1, NYL)
        ])
        if j == 0:
            gate_send(2, gate_take(1))

    for j in range(CHUNKS):
        for copy in ry[j]:
            copy.wait_recv()
        whole = ysum[j, y_lo].astype(F32)
        for d in range(NYL - 1):
            whole = whole + yrx[j, d].astype(F32)
        fin[j] = whole.reshape(2, TM, 2 * CW)
        lo = pl.ds(pl.multiple_of(c * HALF + j * CW, CW), CW)
        for out, part in ((kg_out, slice(0, CW)), (vg_out, slice(CW, 2 * CW))):
            ends.append(remote(fin.at[j, 1 - c, :, part], out.at[:, lo], partner))
            stayed.append(stay(fin.at[j, c, :, part], out.at[:, lo]))

    gate_send(3, gate_take(2))
    row = gate_take(3)
    gg_out[...] = row * (1.0 / math.sqrt(TQ * 512 * HEAD_DIM))

    for copy in ends:
        copy.wait_recv()
    for copy in stayed:
        copy.wait()
    for copy in sent:
        copy.wait_send()


def on_device(queries, keys, memory_values, block_mask, head_gate, out_grad):
    anywhere = pl.BlockSpec(memory_space=pl.ANY)
    vmem = pl.BlockSpec(memory_space=pltpu.VMEM)
    smem = pl.BlockSpec(memory_space=pltpu.SMEM)
    attended, query_gradient, key_gradient, value_gradient, gate = pl.pallas_call(
        kernel,
        out_shape=(
            jax.ShapeDtypeStruct((TQ, FEAT), BF),
            jax.ShapeDtypeStruct((TQ, FEAT), BF),
            jax.ShapeDtypeStruct((TM, FEAT), F32),
            jax.ShapeDtypeStruct((TM, FEAT), F32),
            jax.ShapeDtypeStruct((8, 128), F32),
        ),
        in_specs=[anywhere, anywhere, anywhere, vmem, smem, anywhere],
        out_specs=(anywhere, anywhere, anywhere, anywhere, vmem),
        scratch_shapes=[
            pltpu.VMEM((2, TM, HALF), BF),
            pltpu.VMEM((2, TM, HALF), BF),
            pltpu.VMEM((2, TQ, HALF), BF),
            pltpu.VMEM((2, TQ, HALF), BF),
            pltpu.VMEM((2, 8, 128), F32),
            pltpu.VMEM((MEM, NQ), F32),
            pltpu.VMEM((CHUNKS, CHIPS, ROWS, 2 * CW), BF),
            pltpu.VMEM((2, TQ, HALF), BF),
            pltpu.VMEM((2, TQ, HALF), BF),
            pltpu.VMEM((CHUNKS, CHIPS, ROWS, 2 * CW), BF),
            pltpu.VMEM((CHUNKS, 2, 2, ROWS, 2 * CW), BF),
            pltpu.VMEM((CHUNKS, 2, NYL, ROWS, 2 * CW), BF),
            pltpu.VMEM((CHUNKS, NYL, ROWS, 2 * CW), BF),
            pltpu.VMEM((CHUNKS, NYL - 1, ROWS, 2 * CW), BF),
            pltpu.VMEM((CHUNKS, 2, TM, 2 * CW), F32),
            pltpu.VMEM((NX + NY + NZ + 2, 8, 128), F32),
            pltpu.SemaphoreType.DMA((SEMS,)),
            pltpu.SemaphoreType.DMA((SEMS,)),
            pltpu.SemaphoreType.DMA((16,)),
        ],
        compiler_params=pltpu.CompilerParams(
            collective_id=0, has_side_effects=True, vmem_limit_bytes=40 * 1024 * 1024
        ),
    )(queries, keys, memory_values, block_mask, head_gate, out_grad)
    return attended, query_gradient, key_gradient, value_gradient, gate[0, :HEADS]


def solution(mesh):
    placed = P(("dp", "blk"), None)
    return jax.shard_map(
        on_device,
        mesh=mesh,
        in_specs=(placed, placed, placed, placed, P(), placed),
        out_specs=(placed, placed, placed, placed, P()),
        check_vma=False,
    )
```

```python
import math

import jax
import jax.numpy as jnp
from jax import lax
from jax.experimental import pallas as pl
from jax.experimental.pallas import tpu as pltpu
from jax.sharding import PartitionSpec as P

MESH = pl.DeviceIdType.MESH
HEADS, HEAD_DIM, QBLK = 16, 128, 64
TQ, TM, FEAT = 128, 8, 2048
NX, NY, NZ, NYL = 4, 8, 8, 4
HALF = FEAT // 2
CHUNKS = 4
CH_HEADS = HEADS // 2 // CHUNKS
CW = CH_HEADS * HEAD_DIM
CHIPS = NX * NYL
ROWS = 2 * TM
MEM = CHIPS * ROWS
NQ = 2 * TQ
SEMS = 112
VMEM_BYTES = 64_000_000
BF, F32 = jnp.bfloat16, jnp.float32


def nt(a, b):
    return lax.dot_general(a, b, (((1,), (1,)), ((), ())), preferred_element_type=F32)


def tn(a, b):
    return lax.dot_general(a, b, (((0,), (0,)), ((), ())), preferred_element_type=F32)


def nn(a, b):
    return lax.dot_general(a, b, (((1,), (0,)), ((), ())), preferred_element_type=F32)


def kernel(
    q_ref, k_ref, v_ref, mask_ref, gate_ref, og_ref,
    att_out, qg_out, kg_out, vg_out, gg_out,
    kx, vx, mk, gt, qa, oa, mb, bias, gath, att, qg, term, rxa, rxn, ysum, yrx, fin, gsl, send, recv, local,
):
    dp, blk = lax.axis_index("dp"), lax.axis_index("blk")
    y_hi, z = dp // NZ, dp % NZ
    x, y_lo, c = blk // (2 * NYL), (blk // 2) % NYL, blk % 2
    y = y_hi * NYL + y_lo
    me = x * NYL + y_lo

    def device(x=x, y=y, z=z, c=c):
        return (y // NYL * NZ + z, x * (2 * NYL) + (y % NYL) * 2 + c)

    partner = device(c=1 - c)
    right, left = device(x=(x + 1) % NX), device(x=(x + NX - 1) % NX)
    y_near = [device(y=y_hi * NYL + (y_lo + d) % NYL) for d in range(1, NYL)]
    gate_peers = [
        [device(x=(x + d) % NX) for d in range(1, NX)],
        [device(y=(y + d) % NY) for d in range(1, NY)],
        [device(z=(z + d) % NZ) for d in range(1, NZ)],
        [partner],
    ]

    count = [0, 0]
    sent, stayed = [], []

    def remote(src, dst, to):
        i = count[0]
        count[0] += 1
        copy = pltpu.make_async_remote_copy(
            src_ref=src, dst_ref=dst, send_sem=send.at[i], recv_sem=recv.at[i],
            device_id=to, device_id_type=MESH,
        )
        copy.start()
        sent.append(copy)
        return copy

    def stay(src, dst):
        i = count[1]
        count[1] += 1
        copy = pltpu.make_async_copy(src, dst, local.at[i])
        copy.start()
        return copy

    mine = pl.ds(pl.multiple_of(c * HALF, HALF), HALF)
    other = pl.ds(pl.multiple_of((1 - c) * HALF, HALF), HALF)

    small = [stay(mask_ref, mk), stay(gate_ref, gt)]
    own_kv = [stay(k_ref.at[:, mine], kx.at[c]), stay(v_ref.at[:, mine], vx.at[c])]
    own_q = [stay(q_ref.at[:, mine], qa.at[0]), stay(og_ref.at[:, mine], oa.at[0])]
    mb[0] = jnp.zeros((8, 128), F32)

    barrier = pltpu.get_barrier_semaphore()
    peers = [to for stage in gate_peers for to in stage]
    for to in peers:
        pl.semaphore_signal(barrier, inc=1, device_id=to, device_id_type=MESH)
    pl.semaphore_wait(barrier, len(peers))

    kv_in = [
        remote(k_ref.at[:, other], kx.at[c], partner),
        remote(v_ref.at[:, other], vx.at[c], partner),
    ]
    q_in = [
        remote(q_ref.at[:, other], qa.at[1], partner),
        remote(og_ref.at[:, other], oa.at[1], partner),
    ]

    for copy in small:
        copy.wait()
    mb[0, 0:2, 0 : 2 * CHIPS] = mk[...].astype(F32)
    for copy in own_kv:
        copy.wait()
    for copy in kv_in:
        copy.wait_recv()
    k_rows = kx[...].astype(F32).reshape(ROWS, HALF).astype(BF)
    v_rows = vx[...].astype(F32).reshape(ROWS, HALF).astype(BF)
    for j in range(CHUNKS):
        gath[j, me, :, 0:CW] = k_rows[:, j * CW : (j + 1) * CW]
        gath[j, me, :, CW : 2 * CW] = v_rows[:, j * CW : (j + 1) * CW]

    y_in = [
        [remote(gath.at[j, me], gath.at[j, me], to) for to in y_near] for j in range(CHUNKS)
    ]

    mask_in = remote(mb.at[0], mb.at[1], partner)

    x_of = lambda d: (x + d) % NX
    x_in, far_in = [], []

    def send_x(j):
        for copy in y_in[j]:
            copy.wait_recv()
        block = gath.at[j, pl.ds(x * NYL, NYL)]
        x_in.append([remote(block, block, right), remote(block, block, left)])

    def send_far(j):
        x_in[j][0].wait_recv()
        part = gath.at[j, pl.ds(x_of(3) * NYL, 2)]
        first = remote(part, part, right)
        x_in[j][1].wait_recv()
        part = gath.at[j, pl.ds(x_of(1) * NYL + 2, 2)]
        far_in.append([first, remote(part, part, left)])

    send_x(0)
    send_x(1)
    send_far(0)
    send_x(2)

    mask_in.wait_recv()
    rows = lax.broadcasted_iota(jnp.int32, (MEM, 128), 0) // TM
    lanes = lax.broadcasted_iota(jnp.int32, (MEM, 128), 1)
    pick = jnp.where(rows == lanes, 1.0, 0.0).astype(F32)
    spread = jnp.concatenate(
        [jnp.broadcast_to(mb[s, b : b + 1, :], (QBLK, 128)) for s in range(2) for b in range(2)],
        axis=0,
    )
    bias[...] = (nt(pick.astype(BF), spread.astype(BF)) - 1.0) * 1e30

    send_far(1)
    send_x(3)
    send_far(2)

    for copy in own_q:
        copy.wait()
    for copy in q_in:
        copy.wait_recv()

    scale = 1.0 / math.sqrt(HEAD_DIM)
    lane = lax.broadcasted_iota(jnp.int32, (8, 128), 1)
    gate_row = jnp.zeros((8, 128), F32)
    rx1 = []

    def compute(j, gate_row):
        for copy in far_in[j]:
            copy.wait_recv()
        for h in range(CH_HEADS):
            head = j * CH_HEADS + h
            cols = slice(head * HEAD_DIM, (head + 1) * HEAD_DIM)
            kc = slice(h * HEAD_DIM, (h + 1) * HEAD_DIM)
            vc = slice(CW + h * HEAD_DIM, CW + (h + 1) * HEAD_DIM)
            g = gt[c * (HEADS // 2) + head]
            qh = qa[:, :, cols].reshape(NQ, HEAD_DIM)
            oh = oa[:, :, cols].reshape(NQ, HEAD_DIM)
            kh = gath[j, :, :, kc].reshape(MEM, HEAD_DIM)
            vh = gath[j, :, :, vc].reshape(MEM, HEAD_DIM)
            s = nt(kh, qh) * (scale * math.log2(math.e)) + bias[...]
            e = jnp.exp2(s - jnp.max(s, axis=0, keepdims=True))
            p = e * (1.0 / jnp.sum(e, axis=0, keepdims=True))
            low = p.astype(BF)
            dp_ = nt(vh, oh)
            delta = jnp.sum(low.astype(F32) * dp_, axis=0, keepdims=True)
            ds = (p * (dp_ - delta) * (g * scale)).astype(BF)
            term[j, :, :, kc] = nn(ds, qh).astype(BF).reshape(CHIPS, ROWS, HEAD_DIM)
            term[j, :, :, vc] = (nn(low, oh) * g).astype(BF).reshape(CHIPS, ROWS, HEAD_DIM)
            att[:, :, cols] = (tn(low, vh) * g).astype(BF).reshape(2, TQ, HEAD_DIM)
            qg[:, :, cols] = tn(ds, kh).astype(BF).reshape(2, TQ, HEAD_DIM)
            total = jnp.sum(delta, axis=1, keepdims=True)
            gate_row = gate_row + jnp.where(lane == c * (HEADS // 2) + head, total, 0.0)
        rx1.append([
            remote(term.at[j, pl.ds(x_of(2) * NYL, 2)], rxa.at[j, 0], right),
            remote(term.at[j, pl.ds(x_of(2) * NYL + 2, 2)], rxa.at[j, 1], left),
        ])
        return gate_row

    rx2 = []

    def reduce_x(j):
        rx1[j][0].wait_recv()
        to = pl.ds(x_of(1) * NYL, 2)
        term[j, to] = (term[j, to].astype(F32) + rxa[j, 0].astype(F32)).astype(BF)
        first = remote(term.at[j, pl.ds(x_of(1) * NYL, NYL)], rxn.at[j, 0], right)
        rx1[j][1].wait_recv()
        to = pl.ds(x_of(3) * NYL + 2, 2)
        term[j, to] = (term[j, to].astype(F32) + rxa[j, 1].astype(F32)).astype(BF)
        rx2.append([first, remote(term.at[j, pl.ds(x_of(3) * NYL, NYL)], rxn.at[j, 1], left)])

    gate_slots = [(0, NX, x), (NX, NY, y), (NX + NY, NZ, z), (NX + NY + NZ, 2, c)]
    gate_in = []

    def gate_send(stage, row):
        base, _, at = gate_slots[stage]
        gsl[base + at] = row
        for to in gate_peers[stage]:
            gate_in.append(remote(gsl.at[base + at], gsl.at[base + at], to))

    def gate_take(stage):
        base, size, _ = gate_slots[stage]
        for copy in gate_in:
            copy.wait_recv()
        gate_in.clear()
        row = gsl[base]
        for i in range(1, size):
            row = row + gsl[base + i]
        return row

    ends = []

    def put(src, out, j):
        lo = pl.ds(pl.multiple_of(c * HALF + j * CW, CW), CW)
        part = slice(j * CW, (j + 1) * CW)
        ends.append(remote(src.at[1, :, part], out.at[:, lo], partner))
        stayed.append(stay(src.at[0, :, part], out.at[:, lo]))

    for j in range(CHUNKS):
        gate_row = compute(j, gate_row)
        if j == 0:
            send_far(CHUNKS - 1)
        else:
            put(att, att_out, j - 1)
            put(qg, qg_out, j - 1)
        if j == CHUNKS - 1:
            gate_send(0, gate_row)
        if j > 0:
            reduce_x(j - 1)
    put(att, att_out, CHUNKS - 1)
    put(qg, qg_out, CHUNKS - 1)

    ry = []

    def reduce_y(j):
        for copy in rx2[j]:
            copy.wait_recv()
        own = term[j, pl.ds(x * NYL, NYL)].astype(F32)
        ysum[j] = (own + rxn[j, 0].astype(F32) + rxn[j, 1].astype(F32)).astype(BF)
        ry.append([
            remote(ysum.at[j, (y_lo + d) % NYL], yrx.at[j, d - 1], y_near[d - 1])
            for d in range(1, NYL)
        ])

    reduce_y(0)
    gate_send(1, gate_take(0))
    reduce_y(1)
    reduce_x(CHUNKS - 1)
    reduce_y(2)
    gate_send(2, gate_take(1))
    reduce_y(3)

    for j in range(CHUNKS):
        if j == CHUNKS - 1:
            gate_send(3, gate_take(2))
        for copy in ry[j]:
            copy.wait_recv()
        whole = ysum[j, y_lo].astype(F32)
        for d in range(NYL - 1):
            whole = whole + yrx[j, d].astype(F32)
        fin[j] = whole.reshape(2, TM, 2 * CW)
        lo = pl.ds(pl.multiple_of(c * HALF + j * CW, CW), CW)
        for out, part in ((kg_out, slice(0, CW)), (vg_out, slice(CW, 2 * CW))):
            ends.append(remote(fin.at[j, 1 - c, :, part], out.at[:, lo], partner))
            stayed.append(stay(fin.at[j, c, :, part], out.at[:, lo]))

    row = gate_take(3)
    gg_out[...] = row * (1.0 / math.sqrt(TQ * 512 * HEAD_DIM))

    for copy in ends:
        copy.wait_recv()
    for copy in stayed:
        copy.wait()
    for copy in sent:
        copy.wait_send()


def place(a, b, d, e, g, a_out, b_out, d_out, e_out, g_out, a_buf, b_buf, d_buf, e_buf, g_buf, sems):
    staged = [(a, a_buf, a_out), (b, b_buf, b_out), (d, d_buf, d_out), (e, e_buf, e_out)]
    taken = [
        pltpu.make_async_copy(src, buf, sems.at[i]) for i, (src, buf, _) in enumerate(staged)
    ] + [pltpu.make_async_copy(g, g_buf, sems.at[4])]
    put = [
        pltpu.make_async_copy(buf, dst, sems.at[5 + i]) for i, (_, buf, dst) in enumerate(staged)
    ]
    for copy in taken:
        copy.start()
    for into, out in zip(taken, put):
        into.wait()
        out.start()
    taken[4].wait()
    g_out[...] = g_buf[0, :HEADS]
    for copy in put:
        copy.wait()


def on_device(queries, keys, memory_values, block_mask, head_gate, out_grad):
    anywhere = pl.BlockSpec(memory_space=pl.ANY)
    hbm = pl.BlockSpec(memory_space=pltpu.HBM)
    vmem = pl.BlockSpec(memory_space=pltpu.VMEM)
    results = pl.pallas_call(
        kernel,
        out_shape=(
            jax.ShapeDtypeStruct((TQ, FEAT), BF),
            jax.ShapeDtypeStruct((TQ, FEAT), BF),
            jax.ShapeDtypeStruct((TM, FEAT), F32),
            jax.ShapeDtypeStruct((TM, FEAT), F32),
            jax.ShapeDtypeStruct((8, 128), F32),
        ),
        in_specs=[hbm] * 6,
        out_specs=(anywhere, anywhere, anywhere, anywhere, vmem),
        scratch_shapes=[
            pltpu.VMEM((2, TM, HALF), BF),
            pltpu.VMEM((2, TM, HALF), BF),
            pltpu.VMEM((2, 2 * CHIPS), jnp.int32),
            pltpu.SMEM((HEADS,), F32),
            pltpu.VMEM((2, TQ, HALF), BF),
            pltpu.VMEM((2, TQ, HALF), BF),
            pltpu.VMEM((2, 8, 128), F32),
            pltpu.VMEM((MEM, NQ), F32),
            pltpu.VMEM((CHUNKS, CHIPS, ROWS, 2 * CW), BF),
            pltpu.VMEM((2, TQ, HALF), BF),
            pltpu.VMEM((2, TQ, HALF), BF),
            pltpu.VMEM((CHUNKS, CHIPS, ROWS, 2 * CW), BF),
            pltpu.VMEM((CHUNKS, 2, 2, ROWS, 2 * CW), BF),
            pltpu.VMEM((CHUNKS, 2, NYL, ROWS, 2 * CW), BF),
            pltpu.VMEM((CHUNKS, NYL, ROWS, 2 * CW), BF),
            pltpu.VMEM((CHUNKS, NYL - 1, ROWS, 2 * CW), BF),
            pltpu.VMEM((CHUNKS, 2, TM, 2 * CW), F32),
            pltpu.VMEM((NX + NY + NZ + 2, 8, 128), F32),
            pltpu.SemaphoreType.DMA((SEMS,)),
            pltpu.SemaphoreType.DMA((SEMS,)),
            pltpu.SemaphoreType.DMA((32,)),
        ],
        compiler_params=pltpu.CompilerParams(
            collective_id=0, has_side_effects=True, vmem_limit_bytes=VMEM_BYTES
        ),
    )(queries, keys, memory_values, block_mask, head_gate, out_grad)
    return pl.pallas_call(
        place,
        out_shape=(
            jax.ShapeDtypeStruct((TQ, FEAT), BF),
            jax.ShapeDtypeStruct((TQ, FEAT), BF),
            jax.ShapeDtypeStruct((TM, FEAT), F32),
            jax.ShapeDtypeStruct((TM, FEAT), F32),
            jax.ShapeDtypeStruct((HEADS,), F32),
        ),
        in_specs=[hbm] * 5,
        out_specs=(hbm, hbm, hbm, hbm, vmem),
        scratch_shapes=[
            pltpu.VMEM((TQ, FEAT), BF),
            pltpu.VMEM((TQ, FEAT), BF),
            pltpu.VMEM((TM, FEAT), F32),
            pltpu.VMEM((TM, FEAT), F32),
            pltpu.VMEM((8, 128), F32),
            pltpu.SemaphoreType.DMA((9,)),
        ],
        compiler_params=pltpu.CompilerParams(vmem_limit_bytes=VMEM_BYTES),
    )(*results)


def solution(mesh):
    placed = P(("dp", "blk"), None)
    return jax.shard_map(
        on_device,
        mesh=mesh,
        in_specs=(placed, placed, placed, placed, P(), placed),
        out_specs=(placed, placed, placed, placed, P()),
        check_vma=False,
    )
```

```python
import math

import jax
import jax.numpy as jnp
from jax import lax
from jax.experimental import pallas as pl
from jax.experimental.pallas import tpu as pltpu
from jax.sharding import PartitionSpec as P

MESH = pl.DeviceIdType.MESH
HEADS, HEAD_DIM, QBLK = 16, 128, 64
TQ, TM, FEAT = 128, 8, 2048
NX, NY, NZ, NYL = 4, 8, 8, 4
HALF = FEAT // 2
CHUNKS = 4
CH_HEADS = HEADS // 2 // CHUNKS
CW = CH_HEADS * HEAD_DIM
CHIPS = NX * NYL
ROWS = 2 * TM
MEM = CHIPS * ROWS
NQ = 2 * TQ
SEMS = 144
VMEM_BYTES = 64_000_000
BF, F32 = jnp.bfloat16, jnp.float32


def nt(a, b):
    return lax.dot_general(a, b, (((1,), (1,)), ((), ())), preferred_element_type=F32)


def tn(a, b):
    return lax.dot_general(a, b, (((0,), (0,)), ((), ())), preferred_element_type=F32)


def nn(a, b):
    return lax.dot_general(a, b, (((1,), (0,)), ((), ())), preferred_element_type=F32)


def kernel(
    q_ref, k_ref, v_ref, mask_ref, gate_ref, og_ref,
    att_out, qg_out, kg_out, vg_out, gg_out,
    st, mk, gt, qa, oa, mb, bias, gath, att, qg, term, rxa, rxn, ysum, yrx, fin, gsl, send, recv, local,
):
    dp, blk = lax.axis_index("dp"), lax.axis_index("blk")
    y_hi, z = dp // NZ, dp % NZ
    x, y_lo, c = blk // (2 * NYL), (blk // 2) % NYL, blk % 2
    y = y_hi * NYL + y_lo
    me = x * NYL + y_lo

    def device(x=x, y=y, z=z, c=c):
        return (y // NYL * NZ + z, x * (2 * NYL) + (y % NYL) * 2 + c)

    partner = device(c=1 - c)
    right, left = device(x=(x + 1) % NX), device(x=(x + NX - 1) % NX)
    y_near = [device(y=y_hi * NYL + (y_lo + d) % NYL) for d in range(1, NYL)]
    y_cross = [device(y=y_hi * NYL + (y_lo + d) % NYL, c=1 - c) for d in range(1, NYL)]
    gate_peers = [
        [partner]
        + [device(x=(x + d) % NX, c=o) for d in range(1, NX) for o in (c, 1 - c)],
        [device(y=(y + d) % NY) for d in range(1, NY)],
        [device(z=(z + d) % NZ) for d in range(1, NZ)],
    ]

    count = [0, 0]
    sent, stayed = [], []

    def remote(src, dst, to):
        i = count[0]
        count[0] += 1
        copy = pltpu.make_async_remote_copy(
            src_ref=src, dst_ref=dst, send_sem=send.at[i], recv_sem=recv.at[i],
            device_id=to, device_id_type=MESH,
        )
        copy.start()
        sent.append(copy)
        return copy

    def stay(src, dst):
        i = count[1]
        count[1] += 1
        copy = pltpu.make_async_copy(src, dst, local.at[i])
        copy.start()
        return copy

    mine = pl.ds(pl.multiple_of(c * HALF, HALF), HALF)
    other = pl.ds(pl.multiple_of((1 - c) * HALF, HALF), HALF)

    small = [stay(mask_ref, mk), stay(gate_ref, gt)]
    rows_in = [
        [
            stay(ref.at[:, h * HALF + j * CW : h * HALF + (j + 1) * CW], st.at[h, j, :, at : at + CW])
            for h in range(2)
            for ref, at in ((k_ref, 0), (v_ref, CW))
        ]
        for j in range(CHUNKS)
    ]
    own_q = [stay(q_ref.at[:, mine], qa.at[0]), stay(og_ref.at[:, mine], oa.at[0])]
    mb[0] = jnp.zeros((8, 128), F32)

    barrier = pltpu.get_barrier_semaphore()
    peers = [to for stage in gate_peers for to in stage] + y_cross
    for to in peers:
        pl.semaphore_signal(barrier, inc=1, device_id=to, device_id_type=MESH)
    pl.semaphore_wait(barrier, len(peers))

    def send_y(j):
        for copy in rows_in[j]:
            copy.wait()
        own.append(stay(st.at[c, j], gath.at[j, me, c]))
        taken = [remote(st.at[1 - c, j], gath.at[j, me, c], partner)]
        for same, cross in zip(y_near, y_cross):
            taken.append(remote(st.at[c, j], gath.at[j, me, c], same))
            taken.append(remote(st.at[1 - c, j], gath.at[j, me, c], cross))
        y_in.append(taken)

    own, y_in = [], []
    for j in range(CHUNKS):
        send_y(j)

    q_in = [
        remote(q_ref.at[:, other], qa.at[1], partner),
        remote(og_ref.at[:, other], oa.at[1], partner),
    ]

    for copy in small:
        copy.wait()
    mb[0, 0:2, 0 : 2 * CHIPS] = mk[...].astype(F32)
    mask_in = remote(mb.at[0], mb.at[1], partner)

    x_of = lambda d: (x + d) % NX
    x_in, far_in = [], []

    def send_x(j):
        own[j].wait()
        for copy in y_in[j]:
            copy.wait_recv()
        block = gath.at[j, pl.ds(x * NYL, NYL)]
        x_in.append([remote(block, block, right), remote(block, block, left)])

    def send_far(j):
        x_in[j][0].wait_recv()
        part = gath.at[j, pl.ds(x_of(3) * NYL, 2)]
        first = remote(part, part, right)
        x_in[j][1].wait_recv()
        part = gath.at[j, pl.ds(x_of(1) * NYL + 2, 2)]
        far_in.append([first, remote(part, part, left)])

    send_x(0)
    send_x(1)
    send_far(0)
    send_x(2)

    mask_in.wait_recv()
    rows = lax.broadcasted_iota(jnp.int32, (MEM, 128), 0) // TM
    lanes = lax.broadcasted_iota(jnp.int32, (MEM, 128), 1)
    pick = jnp.where(rows == lanes, 1.0, 0.0).astype(F32)
    spread = jnp.concatenate(
        [jnp.broadcast_to(mb[s, b : b + 1, :], (QBLK, 128)) for s in range(2) for b in range(2)],
        axis=0,
    )
    bias[...] = (nt(pick.astype(BF), spread.astype(BF)) - 1.0) * 1e30

    send_far(1)
    send_x(3)
    send_far(2)

    for copy in own_q:
        copy.wait()
    for copy in q_in:
        copy.wait_recv()

    scale = 1.0 / math.sqrt(HEAD_DIM)
    lane = lax.broadcasted_iota(jnp.int32, (8, 128), 1)
    gate_row = jnp.zeros((8, 128), F32)
    rx1 = []

    def compute(j, gate_row):
        for copy in far_in[j]:
            copy.wait_recv()
        for h in range(CH_HEADS):
            head = j * CH_HEADS + h
            cols = slice(head * HEAD_DIM, (head + 1) * HEAD_DIM)
            kc = slice(h * HEAD_DIM, (h + 1) * HEAD_DIM)
            vc = slice(CW + h * HEAD_DIM, CW + (h + 1) * HEAD_DIM)
            g = gt[c * (HEADS // 2) + head]
            qh = qa[:, :, cols].reshape(NQ, HEAD_DIM)
            oh = oa[:, :, cols].reshape(NQ, HEAD_DIM)
            kh = gath[j, :, :, :, kc].astype(F32).reshape(MEM, HEAD_DIM).astype(BF)
            vh = gath[j, :, :, :, vc].astype(F32).reshape(MEM, HEAD_DIM).astype(BF)
            s = nt(kh, qh) * (scale * math.log2(math.e)) + bias[...]
            e = jnp.exp2(s - jnp.max(s, axis=0, keepdims=True))
            p = e * (1.0 / jnp.sum(e, axis=0, keepdims=True))
            low = p.astype(BF)
            dp_ = nt(vh, oh)
            delta = jnp.sum(low.astype(F32) * dp_, axis=0, keepdims=True)
            ds = (p * (dp_ - delta) * (g * scale)).astype(BF)
            term[j, :, :, :, kc] = nn(ds, qh).reshape(CHIPS, 2, TM, HEAD_DIM).astype(BF)
            term[j, :, :, :, vc] = (nn(low, oh) * g).reshape(CHIPS, 2, TM, HEAD_DIM).astype(BF)
            att[:, :, cols] = (tn(low, vh) * g).astype(BF).reshape(2, TQ, HEAD_DIM)
            qg[:, :, cols] = tn(ds, kh).astype(BF).reshape(2, TQ, HEAD_DIM)
            total = jnp.sum(delta, axis=1, keepdims=True)
            gate_row = gate_row + jnp.where(lane == c * (HEADS // 2) + head, total, 0.0)
        rx1.append([
            remote(term.at[j, pl.ds(x_of(2) * NYL, 2)], rxa.at[j, 0], right),
            remote(term.at[j, pl.ds(x_of(2) * NYL + 2, 2)], rxa.at[j, 1], left),
        ])
        return gate_row

    rx2 = []

    def reduce_x(j):
        rx1[j][0].wait_recv()
        to = pl.ds(x_of(1) * NYL, 2)
        term[j, to] = (term[j, to].astype(F32) + rxa[j, 0].astype(F32)).astype(BF)
        first = remote(term.at[j, pl.ds(x_of(1) * NYL, NYL)], rxn.at[j, 0], right)
        rx1[j][1].wait_recv()
        to = pl.ds(x_of(3) * NYL + 2, 2)
        term[j, to] = (term[j, to].astype(F32) + rxa[j, 1].astype(F32)).astype(BF)
        rx2.append([first, remote(term.at[j, pl.ds(x_of(3) * NYL, NYL)], rxn.at[j, 1], left)])

    gate_slots = [(0, 2 * NX, 2 * x + c), (2 * NX, NY, y), (2 * NX + NY, NZ, z)]
    gate_in = []

    def gate_send(stage, row):
        base, _, at = gate_slots[stage]
        gsl[base + at] = row
        for to in gate_peers[stage]:
            gate_in.append(remote(gsl.at[base + at], gsl.at[base + at], to))

    def gate_take(stage):
        base, size, _ = gate_slots[stage]
        for copy in gate_in:
            copy.wait_recv()
        gate_in.clear()
        row = gsl[base]
        for i in range(1, size):
            row = row + gsl[base + i]
        return row

    ends = []

    def put(src, out, j):
        lo = pl.ds(pl.multiple_of(c * HALF + j * CW, CW), CW)
        part = slice(j * CW, (j + 1) * CW)
        ends.append(remote(src.at[1, :, part], out.at[:, lo], partner))
        stayed.append(stay(src.at[0, :, part], out.at[:, lo]))

    for j in range(CHUNKS):
        gate_row = compute(j, gate_row)
        if j == 0:
            send_far(CHUNKS - 1)
        else:
            put(att, att_out, j - 1)
            put(qg, qg_out, j - 1)
        if j == CHUNKS - 1:
            gate_send(0, gate_row)
        if j > 0:
            reduce_x(j - 1)
    put(att, att_out, CHUNKS - 1)
    put(qg, qg_out, CHUNKS - 1)

    ry = []

    def reduce_y(j):
        for copy in rx2[j]:
            copy.wait_recv()
        own = term[j, pl.ds(x * NYL, NYL)].astype(F32)
        ysum[j] = (own + rxn[j, 0].astype(F32) + rxn[j, 1].astype(F32)).astype(BF)
        taken = [remote(ysum.at[j, y_lo, 1 - c], yrx.at[j, 0, 1], partner)]
        for d in range(1, NYL):
            to = (y_lo + d) % NYL
            taken.append(remote(ysum.at[j, to, c], yrx.at[j, d, 0], y_near[d - 1]))
            taken.append(remote(ysum.at[j, to, 1 - c], yrx.at[j, d, 1], y_cross[d - 1]))
        ry.append(taken)

    reduce_y(0)
    gate_send(1, gate_take(0))
    reduce_y(1)
    reduce_x(CHUNKS - 1)
    reduce_y(2)
    gate_send(2, gate_take(1))
    reduce_y(3)

    for j in range(CHUNKS):
        for copy in ry[j]:
            copy.wait_recv()
        same = ysum[j, y_lo, c].astype(F32)
        cross = yrx[j, 0, 1].astype(F32)
        for d in range(1, NYL):
            same = same + yrx[j, d, 0].astype(F32)
            cross = cross + yrx[j, d, 1].astype(F32)
        for r, (half, whole) in enumerate(((c, same), (1 - c, cross))):
            fin[j, r] = whole
            lo = pl.ds(pl.multiple_of(half * HALF + j * CW, CW), CW)
            for out, part in ((kg_out, slice(0, CW)), (vg_out, slice(CW, 2 * CW))):
                stayed.append(stay(fin.at[j, r, :, part], out.at[:, lo]))

    row = gate_take(2)
    gg_out[...] = row * (1.0 / math.sqrt(TQ * 512 * HEAD_DIM))

    for copy in ends:
        copy.wait_recv()
    for copy in stayed:
        copy.wait()
    for copy in sent:
        copy.wait_send()


def place(a, b, d, e, g, a_out, b_out, d_out, e_out, g_out, a_buf, b_buf, d_buf, e_buf, g_buf, sems):
    staged = [(a, a_buf, a_out), (b, b_buf, b_out), (d, d_buf, d_out), (e, e_buf, e_out)]
    taken = [
        pltpu.make_async_copy(src, buf, sems.at[i]) for i, (src, buf, _) in enumerate(staged)
    ] + [pltpu.make_async_copy(g, g_buf, sems.at[4])]
    put = [
        pltpu.make_async_copy(buf, dst, sems.at[5 + i]) for i, (_, buf, dst) in enumerate(staged)
    ]
    for copy in taken:
        copy.start()
    for into, out in zip(taken, put):
        into.wait()
        out.start()
    taken[4].wait()
    g_out[...] = g_buf[0, :HEADS]
    for copy in put:
        copy.wait()


def on_device(queries, keys, memory_values, block_mask, head_gate, out_grad):
    anywhere = pl.BlockSpec(memory_space=pl.ANY)
    hbm = pl.BlockSpec(memory_space=pltpu.HBM)
    vmem = pl.BlockSpec(memory_space=pltpu.VMEM)
    results = pl.pallas_call(
        kernel,
        out_shape=(
            jax.ShapeDtypeStruct((TQ, FEAT), BF),
            jax.ShapeDtypeStruct((TQ, FEAT), BF),
            jax.ShapeDtypeStruct((TM, FEAT), F32),
            jax.ShapeDtypeStruct((TM, FEAT), F32),
            jax.ShapeDtypeStruct((8, 128), F32),
        ),
        in_specs=[hbm] * 6,
        out_specs=(anywhere, anywhere, anywhere, anywhere, vmem),
        scratch_shapes=[
            pltpu.VMEM((2, CHUNKS, TM, 2 * CW), BF),
            pltpu.VMEM((2, 2 * CHIPS), jnp.int32),
            pltpu.SMEM((HEADS,), F32),
            pltpu.VMEM((2, TQ, HALF), BF),
            pltpu.VMEM((2, TQ, HALF), BF),
            pltpu.VMEM((2, 8, 128), F32),
            pltpu.VMEM((MEM, NQ), F32),
            pltpu.VMEM((CHUNKS, CHIPS, 2, TM, 2 * CW), BF),
            pltpu.VMEM((2, TQ, HALF), BF),
            pltpu.VMEM((2, TQ, HALF), BF),
            pltpu.VMEM((CHUNKS, CHIPS, 2, TM, 2 * CW), BF),
            pltpu.VMEM((CHUNKS, 2, 2, 2, TM, 2 * CW), BF),
            pltpu.VMEM((CHUNKS, 2, NYL, 2, TM, 2 * CW), BF),
            pltpu.VMEM((CHUNKS, NYL, 2, TM, 2 * CW), BF),
            pltpu.VMEM((CHUNKS, NYL, 2, TM, 2 * CW), BF),
            pltpu.VMEM((CHUNKS, 2, TM, 2 * CW), F32),
            pltpu.VMEM((2 * NX + NY + NZ, 8, 128), F32),
            pltpu.SemaphoreType.DMA((SEMS,)),
            pltpu.SemaphoreType.DMA((SEMS,)),
            pltpu.SemaphoreType.DMA((64,)),
        ],
        compiler_params=pltpu.CompilerParams(
            collective_id=0, has_side_effects=True, vmem_limit_bytes=VMEM_BYTES
        ),
    )(queries, keys, memory_values, block_mask, head_gate, out_grad)
    return pl.pallas_call(
        place,
        out_shape=(
            jax.ShapeDtypeStruct((TQ, FEAT), BF),
            jax.ShapeDtypeStruct((TQ, FEAT), BF),
            jax.ShapeDtypeStruct((TM, FEAT), F32),
            jax.ShapeDtypeStruct((TM, FEAT), F32),
            jax.ShapeDtypeStruct((HEADS,), F32),
        ),
        in_specs=[hbm] * 5,
        out_specs=(hbm, hbm, hbm, hbm, vmem),
        scratch_shapes=[
            pltpu.VMEM((TQ, FEAT), BF),
            pltpu.VMEM((TQ, FEAT), BF),
            pltpu.VMEM((TM, FEAT), F32),
            pltpu.VMEM((TM, FEAT), F32),
            pltpu.VMEM((8, 128), F32),
            pltpu.SemaphoreType.DMA((9,)),
        ],
        compiler_params=pltpu.CompilerParams(vmem_limit_bytes=VMEM_BYTES),
    )(*results)


def solution(mesh):
    placed = P(("dp", "blk"), None)
    return jax.shard_map(
        on_device,
        mesh=mesh,
        in_specs=(placed, placed, placed, placed, P(), placed),
        out_specs=(placed, placed, placed, placed, P()),
        check_vma=False,
    )
```

```python
import math

import jax
import jax.numpy as jnp
from jax import lax
from jax.experimental import pallas as pl
from jax.experimental.pallas import tpu as pltpu
from jax.sharding import PartitionSpec as P

MESH = pl.DeviceIdType.MESH
HEADS, HEAD_DIM, QBLK = 16, 128, 64
TQ, TM, FEAT = 128, 8, 2048
NX, NY, NZ, NYL = 4, 8, 8, 4
HALF = FEAT // 2
CHUNKS = 4
CH_HEADS = HEADS // 2 // CHUNKS
CW = CH_HEADS * HEAD_DIM
CHIPS = NX * NYL
ROWS = 2 * TM
MEM = CHIPS * ROWS
NQ = 2 * TQ
SEMS = 144
VMEM_BYTES = 64_000_000
BF, F32 = jnp.bfloat16, jnp.float32


def nt(a, b):
    return lax.dot_general(a, b, (((1,), (1,)), ((), ())), preferred_element_type=F32)


def tn(a, b):
    return lax.dot_general(a, b, (((0,), (0,)), ((), ())), preferred_element_type=F32)


def nn(a, b):
    return lax.dot_general(a, b, (((1,), (0,)), ((), ())), preferred_element_type=F32)


def kernel(
    q_ref, k_ref, v_ref, mask_ref, gate_ref, og_ref,
    att_out, qg_out, kg_out, vg_out, gg_out,
    st, mk, gt, qa, oa, mb, bias, gath, att, qg, term, rxa, rxn, ysum, yrx, fin, gsl, send, recv, local,
):
    dp, blk = lax.axis_index("dp"), lax.axis_index("blk")
    y_hi, z = dp // NZ, dp % NZ
    x, y_lo, c = blk // (2 * NYL), (blk // 2) % NYL, blk % 2
    y = y_hi * NYL + y_lo
    me = x * NYL + y_lo

    def device(x=x, y=y, z=z, c=c):
        return (y // NYL * NZ + z, x * (2 * NYL) + (y % NYL) * 2 + c)

    partner = device(c=1 - c)
    right, left = device(x=(x + 1) % NX), device(x=(x + NX - 1) % NX)
    y_near = [device(y=y_hi * NYL + (y_lo + d) % NYL) for d in range(1, NYL)]
    y_cross = [device(y=y_hi * NYL + (y_lo + d) % NYL, c=1 - c) for d in range(1, NYL)]
    gate_peers = [
        [partner]
        + [device(x=(x + d) % NX, c=o) for d in range(1, NX) for o in (c, 1 - c)],
        [device(y=(y + d) % NY) for d in range(1, NY)],
        [device(z=(z + d) % NZ) for d in range(1, NZ)],
    ]

    count = [0, 0]
    sent, stayed = [], []

    def remote(src, dst, to):
        i = count[0]
        count[0] += 1
        copy = pltpu.make_async_remote_copy(
            src_ref=src, dst_ref=dst, send_sem=send.at[i], recv_sem=recv.at[i],
            device_id=to, device_id_type=MESH,
        )
        copy.start()
        sent.append(copy)
        return copy

    def stay(src, dst):
        i = count[1]
        count[1] += 1
        copy = pltpu.make_async_copy(src, dst, local.at[i])
        copy.start()
        return copy

    mine = pl.ds(pl.multiple_of(c * HALF, HALF), HALF)
    other = pl.ds(pl.multiple_of((1 - c) * HALF, HALF), HALF)

    small = [stay(mask_ref, mk), stay(gate_ref, gt)]
    rows_in = [
        [
            stay(ref.at[:, h * HALF + j * CW : h * HALF + (j + 1) * CW], st.at[h, j, :, at : at + CW])
            for h in range(2)
            for ref, at in ((k_ref, 0), (v_ref, CW))
        ]
        for j in range(CHUNKS)
    ]
    own_q = [stay(q_ref.at[:, mine], qa.at[0]), stay(og_ref.at[:, mine], oa.at[0])]
    mb[0] = jnp.zeros((8, 128), F32)

    barrier = pltpu.get_barrier_semaphore()
    peers = [to for stage in gate_peers for to in stage] + y_cross
    for to in peers:
        pl.semaphore_signal(barrier, inc=1, device_id=to, device_id_type=MESH)
    pl.semaphore_wait(barrier, len(peers))

    def send_y(j):
        for copy in rows_in[j]:
            copy.wait()
        own.append(stay(st.at[c, j], gath.at[j, me, c]))
        taken = []
        for i in (1, 2, 0):
            taken.append(remote(st.at[c, j], gath.at[j, me, c], y_near[i]))
            taken.append(remote(st.at[1 - c, j], gath.at[j, me, c], y_cross[i]))
        taken.append(remote(st.at[1 - c, j], gath.at[j, me, c], partner))
        y_in.append(taken)

    own, y_in = [], []
    for j in range(CHUNKS):
        send_y(j)

    q_in = [
        remote(q_ref.at[:, other], qa.at[1], partner),
        remote(og_ref.at[:, other], oa.at[1], partner),
    ]

    for copy in small:
        copy.wait()
    mb[0, 0:2, 0 : 2 * CHIPS] = mk[...].astype(F32)
    mask_in = remote(mb.at[0], mb.at[1], partner)

    x_of = lambda d: (x + d) % NX
    x_in, far_in = [], []

    def send_x(j):
        own[j].wait()
        for copy in y_in[j]:
            copy.wait_recv()
        block = gath.at[j, pl.ds(x * NYL, NYL)]
        x_in.append([remote(block, block, right), remote(block, block, left)])

    def send_far(j):
        x_in[j][0].wait_recv()
        part = gath.at[j, pl.ds(x_of(3) * NYL, 2)]
        first = remote(part, part, right)
        x_in[j][1].wait_recv()
        part = gath.at[j, pl.ds(x_of(1) * NYL + 2, 2)]
        far_in.append([first, remote(part, part, left)])

    send_x(0)
    send_x(1)
    send_far(0)
    send_x(2)

    mask_in.wait_recv()
    rows = lax.broadcasted_iota(jnp.int32, (MEM, 128), 0) // TM
    lanes = lax.broadcasted_iota(jnp.int32, (MEM, 128), 1)
    pick = jnp.where(rows == lanes, 1.0, 0.0).astype(F32)
    spread = jnp.concatenate(
        [jnp.broadcast_to(mb[s, b : b + 1, :], (QBLK, 128)) for s in range(2) for b in range(2)],
        axis=0,
    )
    bias[...] = (nt(pick.astype(BF), spread.astype(BF)) - 1.0) * 1e30

    send_far(1)
    send_x(3)
    send_far(2)

    for copy in own_q:
        copy.wait()
    for copy in q_in:
        copy.wait_recv()

    scale = 1.0 / math.sqrt(HEAD_DIM)
    lane = lax.broadcasted_iota(jnp.int32, (8, 128), 1)
    gate_row = jnp.zeros((8, 128), F32)
    rx1 = []

    def compute(j, gate_row):
        for copy in far_in[j]:
            copy.wait_recv()
        for h in range(CH_HEADS):
            head = j * CH_HEADS + h
            cols = slice(head * HEAD_DIM, (head + 1) * HEAD_DIM)
            kc = slice(h * HEAD_DIM, (h + 1) * HEAD_DIM)
            vc = slice(CW + h * HEAD_DIM, CW + (h + 1) * HEAD_DIM)
            g = gt[c * (HEADS // 2) + head]
            qh = qa[:, :, cols].reshape(NQ, HEAD_DIM)
            oh = oa[:, :, cols].reshape(NQ, HEAD_DIM)
            kh = gath[j, :, :, :, kc].astype(F32).reshape(MEM, HEAD_DIM).astype(BF)
            vh = gath[j, :, :, :, vc].astype(F32).reshape(MEM, HEAD_DIM).astype(BF)
            s = nt(kh, qh) * (scale * math.log2(math.e)) + bias[...]
            e = jnp.exp2(s - jnp.max(s, axis=0, keepdims=True))
            p = e * (1.0 / jnp.sum(e, axis=0, keepdims=True))
            low = p.astype(BF)
            dp_ = nt(vh, oh)
            delta = jnp.sum(low.astype(F32) * dp_, axis=0, keepdims=True)
            ds = (p * (dp_ - delta) * (g * scale)).astype(BF)
            term[j, :, :, :, kc] = nn(ds, qh).reshape(CHIPS, 2, TM, HEAD_DIM).astype(BF)
            term[j, :, :, :, vc] = (nn(low, oh) * g).reshape(CHIPS, 2, TM, HEAD_DIM).astype(BF)
            att[:, :, cols] = (tn(low, vh) * g).astype(BF).reshape(2, TQ, HEAD_DIM)
            qg[:, :, cols] = tn(ds, kh).astype(BF).reshape(2, TQ, HEAD_DIM)
            total = jnp.sum(delta, axis=1, keepdims=True)
            gate_row = gate_row + jnp.where(lane == c * (HEADS // 2) + head, total, 0.0)
        rx1.append([
            remote(term.at[j, pl.ds(x_of(2) * NYL, 2)], rxa.at[j, 0], right),
            remote(term.at[j, pl.ds(x_of(2) * NYL + 2, 2)], rxa.at[j, 1], left),
        ])
        return gate_row

    rx2 = []

    def reduce_x(j):
        rx1[j][0].wait_recv()
        to = pl.ds(x_of(1) * NYL, 2)
        term[j, to] = (term[j, to].astype(F32) + rxa[j, 0].astype(F32)).astype(BF)
        first = remote(term.at[j, pl.ds(x_of(1) * NYL, NYL)], rxn.at[j, 0], right)
        rx1[j][1].wait_recv()
        to = pl.ds(x_of(3) * NYL + 2, 2)
        term[j, to] = (term[j, to].astype(F32) + rxa[j, 1].astype(F32)).astype(BF)
        rx2.append([first, remote(term.at[j, pl.ds(x_of(3) * NYL, NYL)], rxn.at[j, 1], left)])

    gate_slots = [(0, 2 * NX, 2 * x + c), (2 * NX, NY, y), (2 * NX + NY, NZ, z)]
    gate_in = []

    def gate_send(stage, row):
        base, _, at = gate_slots[stage]
        gsl[base + at] = row
        for to in gate_peers[stage]:
            gate_in.append(remote(gsl.at[base + at], gsl.at[base + at], to))

    def gate_take(stage):
        base, size, _ = gate_slots[stage]
        for copy in gate_in:
            copy.wait_recv()
        gate_in.clear()
        row = gsl[base]
        for i in range(1, size):
            row = row + gsl[base + i]
        return row

    ends = []

    def put(src, out, j):
        lo = pl.ds(pl.multiple_of(c * HALF + j * CW, CW), CW)
        part = slice(j * CW, (j + 1) * CW)
        ends.append(remote(src.at[1, :, part], out.at[:, lo], partner))
        stayed.append(stay(src.at[0, :, part], out.at[:, lo]))

    for j in range(CHUNKS):
        gate_row = compute(j, gate_row)
        if j == 0:
            send_far(CHUNKS - 1)
        else:
            put(att, att_out, j - 1)
            put(qg, qg_out, j - 1)
        if j == CHUNKS - 1:
            gate_send(0, gate_row)
        if j > 0:
            reduce_x(j - 1)
    put(att, att_out, CHUNKS - 1)
    put(qg, qg_out, CHUNKS - 1)

    ry = []

    def reduce_y(j):
        for copy in rx2[j]:
            copy.wait_recv()
        own = term[j, pl.ds(x * NYL, NYL)].astype(F32)
        ysum[j] = (own + rxn[j, 0].astype(F32) + rxn[j, 1].astype(F32)).astype(BF)
        taken = [remote(ysum.at[j, y_lo, 1 - c], yrx.at[j, 0, 1], partner)]
        for d in (2, 3, 1):
            to = (y_lo + d) % NYL
            taken.append(remote(ysum.at[j, to, c], yrx.at[j, d, 0], y_near[d - 1]))
            taken.append(remote(ysum.at[j, to, 1 - c], yrx.at[j, d, 1], y_cross[d - 1]))
        ry.append(taken)

    reduce_y(0)
    gate_send(1, gate_take(0))
    reduce_y(1)
    reduce_x(CHUNKS - 1)
    reduce_y(2)
    gate_send(2, gate_take(1))
    reduce_y(3)

    for j in range(CHUNKS):
        for copy in ry[j]:
            copy.wait_recv()
        same = ysum[j, y_lo, c].astype(F32)
        cross = yrx[j, 0, 1].astype(F32)
        for d in range(1, NYL):
            same = same + yrx[j, d, 0].astype(F32)
            cross = cross + yrx[j, d, 1].astype(F32)
        for r, (half, whole) in enumerate(((c, same), (1 - c, cross))):
            fin[j, r] = whole
            lo = pl.ds(pl.multiple_of(half * HALF + j * CW, CW), CW)
            for out, part in ((kg_out, slice(0, CW)), (vg_out, slice(CW, 2 * CW))):
                stayed.append(stay(fin.at[j, r, :, part], out.at[:, lo]))

    row = gate_take(2)
    gg_out[...] = row * (1.0 / math.sqrt(TQ * 512 * HEAD_DIM))

    for copy in ends:
        copy.wait_recv()
    for copy in stayed:
        copy.wait()
    for copy in sent:
        copy.wait_send()


def place(a, b, d, e, g, a_out, b_out, d_out, e_out, g_out, a_buf, b_buf, d_buf, e_buf, g_buf, sems):
    staged = [(a, a_buf, a_out), (b, b_buf, b_out), (d, d_buf, d_out), (e, e_buf, e_out)]
    taken = [
        pltpu.make_async_copy(src, buf, sems.at[i]) for i, (src, buf, _) in enumerate(staged)
    ] + [pltpu.make_async_copy(g, g_buf, sems.at[4])]
    put = [
        pltpu.make_async_copy(buf, dst, sems.at[5 + i]) for i, (_, buf, dst) in enumerate(staged)
    ]
    for copy in taken:
        copy.start()
    for into, out in zip(taken, put):
        into.wait()
        out.start()
    taken[4].wait()
    g_out[...] = g_buf[0, :HEADS]
    for copy in put:
        copy.wait()


def on_device(queries, keys, memory_values, block_mask, head_gate, out_grad):
    anywhere = pl.BlockSpec(memory_space=pl.ANY)
    hbm = pl.BlockSpec(memory_space=pltpu.HBM)
    vmem = pl.BlockSpec(memory_space=pltpu.VMEM)
    results = pl.pallas_call(
        kernel,
        out_shape=(
            jax.ShapeDtypeStruct((TQ, FEAT), BF),
            jax.ShapeDtypeStruct((TQ, FEAT), BF),
            jax.ShapeDtypeStruct((TM, FEAT), F32),
            jax.ShapeDtypeStruct((TM, FEAT), F32),
            jax.ShapeDtypeStruct((8, 128), F32),
        ),
        in_specs=[hbm] * 6,
        out_specs=(anywhere, anywhere, anywhere, anywhere, vmem),
        scratch_shapes=[
            pltpu.VMEM((2, CHUNKS, TM, 2 * CW), BF),
            pltpu.VMEM((2, 2 * CHIPS), jnp.int32),
            pltpu.SMEM((HEADS,), F32),
            pltpu.VMEM((2, TQ, HALF), BF),
            pltpu.VMEM((2, TQ, HALF), BF),
            pltpu.VMEM((2, 8, 128), F32),
            pltpu.VMEM((MEM, NQ), F32),
            pltpu.VMEM((CHUNKS, CHIPS, 2, TM, 2 * CW), BF),
            pltpu.VMEM((2, TQ, HALF), BF),
            pltpu.VMEM((2, TQ, HALF), BF),
            pltpu.VMEM((CHUNKS, CHIPS, 2, TM, 2 * CW), BF),
            pltpu.VMEM((CHUNKS, 2, 2, 2, TM, 2 * CW), BF),
            pltpu.VMEM((CHUNKS, 2, NYL, 2, TM, 2 * CW), BF),
            pltpu.VMEM((CHUNKS, NYL, 2, TM, 2 * CW), BF),
            pltpu.VMEM((CHUNKS, NYL, 2, TM, 2 * CW), BF),
            pltpu.VMEM((CHUNKS, 2, TM, 2 * CW), F32),
            pltpu.VMEM((2 * NX + NY + NZ, 8, 128), F32),
            pltpu.SemaphoreType.DMA((SEMS,)),
            pltpu.SemaphoreType.DMA((SEMS,)),
            pltpu.SemaphoreType.DMA((64,)),
        ],
        compiler_params=pltpu.CompilerParams(
            collective_id=0, has_side_effects=True, vmem_limit_bytes=VMEM_BYTES
        ),
    )(queries, keys, memory_values, block_mask, head_gate, out_grad)
    return pl.pallas_call(
        place,
        out_shape=(
            jax.ShapeDtypeStruct((TQ, FEAT), BF),
            jax.ShapeDtypeStruct((TQ, FEAT), BF),
            jax.ShapeDtypeStruct((TM, FEAT), F32),
            jax.ShapeDtypeStruct((TM, FEAT), F32),
            jax.ShapeDtypeStruct((HEADS,), F32),
        ),
        in_specs=[hbm] * 5,
        out_specs=(hbm, hbm, hbm, hbm, vmem),
        scratch_shapes=[
            pltpu.VMEM((TQ, FEAT), BF),
            pltpu.VMEM((TQ, FEAT), BF),
            pltpu.VMEM((TM, FEAT), F32),
            pltpu.VMEM((TM, FEAT), F32),
            pltpu.VMEM((8, 128), F32),
            pltpu.SemaphoreType.DMA((9,)),
        ],
        compiler_params=pltpu.CompilerParams(vmem_limit_bytes=VMEM_BYTES),
    )(*results)


def solution(mesh):
    placed = P(("dp", "blk"), None)
    return jax.shard_map(
        on_device,
        mesh=mesh,
        in_specs=(placed, placed, placed, placed, P(), placed),
        out_specs=(placed, placed, placed, placed, P()),
        check_vma=False,
    )
```
